32 devices in a mesh: dp: 8 (over y, x, core), seq: 4 (over z).
Axes of the slice: x: 2, y: 2, z: 4, core: 2. Of those that a mesh axis runs over, the one named last changes fastest.
Arguments:
- queries: bfloat16 [16, 256, 5120], P('dp', 'seq'), may hold values from -50 to 50
- key_rows: bfloat16 [16, 256, 1024], P('dp', 'seq'), may hold values from -6 to 6
- value_rows: bfloat16 [16, 256, 1024], P('dp', 'seq'), may hold values from -6 to 6
- cotangent: bfloat16 [16, 256, 5120], P('dp', 'seq'), may hold values from -6 to 6
- episodes: int32 [16, 256], P('dp', 'seq'), may hold values from 0 to 7, never falling along the last dimension, each value on 1 to 170 neighbouring positions
- send_slot: int32 [8], P('dp'), may hold values from 0 to 1
- swap_mask: int32 [1], replicated, may hold values from 1 to 7
Outputs:
- grad_queries: bfloat16 [16, 256, 5120], P('dp', 'seq')
- grad_keys: bfloat16 [16, 256, 1024], P('dp', 'seq')
- grad_values: bfloat16 [16, 256, 1024], P('dp', 'seq')
The draws below stay inside these ranges and needn't reach their ends.
Inputs may be any that keep to these rules, and one draw needn't show every extreme that they name: `episodes`: episode ids never fall along a span.
All inputs are finite; a program needn't handle non-finite values.
Results may differ from the reference program's by a relative error of at most 0.0055.
Values may be sent and summed in bfloat16 or wider, within the bound.
A program may use at most 64 MiB of HBM per device.

```python
import math
import jax
import jax.numpy as jnp
import numpy as np
from jax import lax

H = 40
KVH = 8
DH = 128
SPANS = 2
EPIS = 8
SPAN_LEN = 256
MOST = 170
ALL_SPANS = 16
N_DP = 8


def paired_draw(key):
    first, second = jax.random.split(jax.random.fold_in(key, 17), 2)
    groups = H // KVH
    query_part = jnp.clip(jax.random.normal(first, (ALL_SPANS, SPAN_LEN, KVH, groups, DH), jnp.float32), -6.0, 6.0)
    key_part = jnp.clip(jax.random.normal(second, (ALL_SPANS, SPAN_LEN, KVH, DH), jnp.float32), -6.0, 6.0)
    return (query_part.reshape(ALL_SPANS, SPAN_LEN, H * DH), key_part.reshape(ALL_SPANS, SPAN_LEN, KVH * DH))


def draw_queries(key, part):
    return paired_draw(key)[0].astype(jnp.bfloat16)


def draw_key_rows(key, part):
    return paired_draw(key)[1].astype(jnp.bfloat16)


def set_ends(values, rng, low, top_value):
    longest = values.shape.index(max(values.shape))
    spots = []
    for shift in (0, 1):
        where = [jax.random.randint(jax.random.fold_in(rng, axis), (), 0, length) for axis, length in enumerate(values.shape)]
        where[longest] = (where[longest] + shift) % values.shape[longest]
        spots.append(tuple(where))
    return values.at[spots[0]].set(low).at[spots[1]].set(top_value)


def level_of(key, shape, pieces, least, high):
    def one(dim, shards_of):
        steps = jax.random.uniform(jax.random.fold_in(jax.random.fold_in(key, 6), dim), (shards_of,), jnp.float32, least / len(pieces), high / len(pieces))
        return jnp.repeat(jnp.exp(steps), shape[dim] // shards_of).reshape((-1,) + (1,) * (len(shape) - dim - 1))

    loudness = one(*pieces[0])
    for cut in pieces[1:]:
        loudness = loudness * one(*cut)
    return loudness


def split_up(count, total, limit, slope):
    portions = [(1 << 20) // math.isqrt(standing ** slope) + 1 for standing in range(2, count + 1)]
    surplus, given = total - limit - (count - 1), [1] * (count - 1)
    while surplus > 0:
        movable = [i for i in range(count - 1) if given[i] < limit]
        pool, left = sum([portions[i] for i in movable]), surplus
        for i in movable:
            more = min(limit - given[i], max(1, left * portions[i] // pool), surplus)
            given[i] = given[i] + more
            surplus = surplus - more
    return np.array([limit] + given)


def ragged(rng, count, total, reach, lean):
    if count == 2:
        one = jax.random.randint(rng, (), max(1, total - reach), min(reach, total - 1) + 1)
        return jnp.stack([one, total - one])
    tallies = jnp.asarray(split_up(count, total, reach, lean), jnp.int32)
    couples = (count - 1) // 2
    donor, receiver = tallies[1:1 + 2 * couples:2], tallies[2:2 + 2 * couples:2]
    room = jnp.minimum(donor - 1, reach - receiver)
    moved = jax.random.randint(jax.random.fold_in(rng, 1), (couples,), 0, 1 << 20) % (room + 1)
    tallies = tallies.at[1:1 + 2 * couples:2].set(donor - moved).at[2:2 + 2 * couples:2].set(receiver + moved)
    return tallies[jax.random.permutation(jax.random.fold_in(rng, 2), count)]


def bell_draw(own_key, extent, deviation, bound, pieces=(), held_as=jnp.bfloat16):
    loudness = level_of(own_key, extent, pieces, -0.22, 0.18) if pieces else 1.0
    values = jax.random.normal(own_key, extent, jnp.float32) * deviation * loudness
    return jnp.minimum(jnp.maximum(values, -bound), bound).astype(held_as)


def setup_inputs(seed: int = 0) -> dict:
    key_list = jax.random.split(jax.random.key(seed), 8)
    return {
        "queries": draw_queries(jax.random.fold_in(key_list[7], 71), 0),
        "key_rows": draw_key_rows(jax.random.fold_in(key_list[7], 71), 0),
        "value_rows": bell_draw(key_list[2], (ALL_SPANS, SPAN_LEN, KVH * DH), 1.0, 6.0, ((0, 8), (1, 4))),
        "cotangent": bell_draw(key_list[3], (ALL_SPANS, SPAN_LEN, H * DH), 1.0, 6.0, ((0, 8), (1, 4))),
        "episodes": jax.vmap(lambda own: jnp.searchsorted(jnp.cumsum(ragged(own, EPIS, SPAN_LEN, MOST, 2)), jnp.arange(SPAN_LEN), side="right"))(jax.random.split(key_list[4], ALL_SPANS)).reshape((ALL_SPANS, SPAN_LEN)).astype(jnp.int32),
        "send_slot": set_ends(jax.random.randint(key_list[5], (N_DP,), 0, 2), jax.random.fold_in(key_list[5], 1), 0, 1).astype(jnp.int32),
        "swap_mask": jax.random.randint(key_list[6], (1,), 1, N_DP).astype(jnp.int32),
    }


def head_group(query_group, key_head, value_head, grad_group, episode_ids):
    scaling = 1.0 / jnp.sqrt(jnp.float32(DH))
    query_full = query_group.astype(jnp.float32)
    key_full = key_head.astype(jnp.float32)
    value_full = value_head.astype(jnp.float32)
    grad_full = grad_group.astype(jnp.float32)
    scores = jnp.einsum('qgd,td->gqt', query_full, key_full) * scaling
    positions = jnp.arange(SPAN_LEN, dtype=jnp.int32)
    allowed = (episode_ids[:, None] == episode_ids[None, :]) & (positions[:, None] >= positions[None, :])
    scores = jnp.where(allowed[None], scores, jnp.float32(-1e+30))
    top = lax.optimization_barrier(jnp.max(scores, axis=-1, keepdims=True))
    expo = jnp.exp(scores - top)
    probs = expo / lax.optimization_barrier(jnp.sum(expo, axis=-1, keepdims=True))
    probs_low = lax.optimization_barrier(probs.astype(jnp.bfloat16)).astype(jnp.float32)
    dprobs = jnp.einsum('qgd,td->gqt', grad_full, value_full)
    delta = lax.optimization_barrier(jnp.sum(probs * dprobs, axis=-1, keepdims=True))
    dscores = lax.optimization_barrier((probs * (dprobs - delta)).astype(jnp.bfloat16)).astype(jnp.float32)
    grad_value = jnp.einsum('gqt,qgd->td', probs_low, grad_full).astype(jnp.bfloat16)
    grad_query = (jnp.einsum('gqt,td->qgd', dscores, key_full) * scaling).astype(jnp.bfloat16)
    grad_key = (jnp.einsum('gqt,qgd->td', dscores, query_full) * scaling).astype(jnp.bfloat16)
    return (grad_query, grad_key, grad_value)

def span_grads(packed):
    query_span, key_span, value_span, grad_span, episode_ids = packed
    groups = H // KVH
    query_heads = query_span.reshape(SPAN_LEN, KVH, groups, DH).transpose(1, 0, 2, 3)
    grad_heads = grad_span.reshape(SPAN_LEN, KVH, groups, DH).transpose(1, 0, 2, 3)
    key_heads = key_span.reshape(SPAN_LEN, KVH, DH).transpose(1, 0, 2)
    value_heads = value_span.reshape(SPAN_LEN, KVH, DH).transpose(1, 0, 2)

    def per_head(packed_group):
        return head_group(packed_group[0], packed_group[1], packed_group[2], packed_group[3], episode_ids)
    grad_query, grad_key, grad_value = lax.map(per_head, (query_heads, key_heads, value_heads, grad_heads))
    grad_query = grad_query.transpose(1, 0, 2, 3).reshape(SPAN_LEN, H * DH)
    grad_key = grad_key.transpose(1, 0, 2).reshape(SPAN_LEN, KVH * DH)
    grad_value = grad_value.transpose(1, 0, 2).reshape(SPAN_LEN, KVH * DH)
    return (grad_query, grad_key, grad_value)

def reference(queries, key_rows, value_rows, cotangent, episodes, send_slot, swap_mask):
    grad_query, grad_key, grad_value = lax.map(span_grads, (queries, key_rows, value_rows, cotangent, episodes))
    replicas = jnp.arange(N_DP, dtype=jnp.int32)
    partner = jnp.bitwise_xor(replicas, swap_mask[0]).astype(jnp.int32)
    kept_index = replicas * SPANS + 1 - send_slot
    taken_index = partner * SPANS + send_slot[partner]
    order = jnp.stack([kept_index, taken_index], axis=1).reshape(-1).astype(jnp.int32)
    return (grad_query[order], grad_key[order], grad_value[order])
```

```python
import functools

import jax
import jax.numpy as jnp
from jax import lax
from jax.experimental import pallas as pl
from jax.experimental.pallas import tpu as pltpu
from jax.sharding import PartitionSpec as P

DH = 128
HP = 2
LAG = 2
AHEAD = 2
OWN = 1
MESH = pl.DeviceIdType.MESH
NT = (((1,), (1,)), ((), ()))
NN = (((1,), (0,)), ((), ()))
TN = (((0,), (0,)), ((), ()))


def dot(a, b, dims):
    return lax.dot_general(a, b, dims, preferred_element_type=jnp.float32)


def kernel(
    n, ndp, mask, send_hbm, ep_hbm, q_hbm, k_hbm, v_hbm, do_hbm,
    gq_out, gk_out, gv_out,
    send_ref, ep_ref, q_ref, k_ref, v_ref, do_ref, load_sem, keep_sem, kvbuf, epbuf, allow, gpart, gown, grecv, tq, tk, tv,
    up_send, up_recv, ep_send, ep_recv, down_send, down_recv, trade_send, trade_recv,
):
    r = lax.axis_index("dp")
    s = lax.axis_index("seq")
    rows = q_ref.shape[1]
    heads = k_ref.shape[2] // DH
    groups = q_ref.shape[2] // k_ref.shape[2]
    per = heads // HP
    pieces = 2 * per
    keys = n * rows
    wide = groups * rows
    scaling = 1.0 / jnp.sqrt(jnp.float32(DH))
    partner = r
    for b in range(ndp.bit_length() - 1):
        if (mask >> b) & 1:
            partner = partner + (1 << b) * (1 - 2 * ((r // (1 << b)) % 2))
    most = 2 * n * rows // 3

    def first(d):
        return min(max(0, d * rows - most + 1) // 16 * 16, rows)

    reach = [d for d in range(1, n) if first(d) < rows]
    own = pl.ds(pl.multiple_of(s * rows, rows), rows)

    barrier = pltpu.get_barrier_semaphore()
    for d in range(1, n):
        pl.semaphore_signal(barrier, inc=1, device_id=(r, (s + d) % n), device_id_type=MESH)
    pl.semaphore_signal(barrier, inc=1, device_id=(partner, s), device_id_type=MESH)
    loads = [
        pltpu.make_async_copy(src, dst, load_sem.at[i])
        for i, (src, dst) in enumerate(
            (
                (send_hbm, send_ref), (ep_hbm, ep_ref), (k_hbm, k_ref), (v_hbm, v_ref),
                (q_hbm, q_ref), (do_hbm, do_ref),
            )
        )
    ]
    for load in loads[:4]:
        load.start()
    for load in loads[:4]:
        load.wait()
    handed = send_ref[0]

    def slot(c):
        return handed + c * (1 - 2 * handed)

    for c in range(2):
        epbuf[s, c:c + 1, 0:rows] = jnp.where(
            slot(c) == 0, ep_ref[0:1, :], ep_ref[1:2, :]
        )
        for g in range(heads):
            kvbuf[c, g, own, 0:DH] = k_ref[slot(c), :, g * DH:(g + 1) * DH]
            kvbuf[c, g, own, DH:2 * DH] = v_ref[slot(c), :, g * DH:(g + 1) * DH]
    for load in loads[4:]:
        load.start()
    pl.semaphore_wait(barrier, n)

    def chunk(t, low=0):
        return pl.ds(pl.multiple_of(t * rows + low, 16), rows - low)

    def up(p, t, d):
        part = kvbuf.at[p // per, pl.ds((p % per) * HP, HP), chunk(t, first(d)), :]
        return pltpu.make_async_remote_copy(
            src_ref=part, dst_ref=part,
            send_sem=up_send.at[p, t], recv_sem=up_recv.at[p, t],
            device_id=(r, (s + 1) % n), device_id_type=MESH,
        )

    def ep_copy(src, dst):
        return pltpu.make_async_remote_copy(
            src_ref=epbuf.at[src], dst_ref=epbuf.at[src],
            send_sem=ep_send.at[dst], recv_sem=ep_recv.at[src],
            device_id=(r, dst), device_id_type=MESH,
        )

    def down(p, t, d):
        c, g = p // per, (p % per) * HP
        part = (c, pl.ds(g, HP), chunk(t, first(d)))
        return pltpu.make_async_remote_copy(
            src_ref=gpart.at[part], dst_ref=grecv.at[part],
            send_sem=down_send.at[p, t], recv_sem=down_recv.at[p, t],
            device_id=(r, (s + n - 1) % n), device_id_type=MESH,
        )

    def trade(which, p, buf, out, width):
        cols = pl.ds(pl.multiple_of(p * HP * width, HP * width), HP * width)
        return pltpu.make_async_remote_copy(
            src_ref=buf.at[0, :, cols], dst_ref=out.at[1, :, cols],
            send_sem=trade_send.at[which, p], recv_sem=trade_recv.at[which, p],
            device_id=(partner, s), device_id_type=MESH,
        )

    def keep(which, p, buf, out, width):
        cols = pl.ds(pl.multiple_of(p * HP * width, HP * width), HP * width)
        return pltpu.make_async_copy(
            buf.at[1, :, cols], out.at[0, :, cols], keep_sem.at[which, p]
        )

    for t in range(n - 1, 0, -1):
        @pl.when(t > s)
        def _(t=t):
            ep_copy(s, t).start()

    def send_own(p):
        @pl.when((s < n - 1) & (p < pieces))
        def _():
            up(p, s, 1).start()

    for p in range(OWN):
        send_own(p)

    def clear(t, size):
        def one(i, carry):
            kvbuf[i // heads, i % heads, pl.ds(pl.multiple_of(t * rows, rows), size), :] = (
                jnp.zeros((size, 2 * DH), jnp.bfloat16)
            )
            return carry

        lax.fori_loop(0, 2 * heads, one, 0)

    for t in range(n):
        @pl.when(t > s)
        def _(t=t):
            epbuf[t, :, :] = jnp.full((8, DH), -1, jnp.int32)
            clear(t, rows)
    for d in range(1, n):
        if first(d) > 0:
            @pl.when(s >= d)
            def _(d=d):
                clear(s - d, first(d))

    for t in range(n - 1):
        @pl.when(t < s)
        def _(t=t):
            ep_copy(t, s).wait_recv()

    eye = lax.broadcasted_iota(jnp.int32, (rows, DH), 0) == lax.broadcasted_iota(
        jnp.int32, (rows, DH), 1
    )
    for c in range(2):
        mine = epbuf[s, c:c + 1, 0:rows]
        mine = jnp.concatenate([mine] * groups, axis=1)
        pos_q = jnp.concatenate(
            [s * rows + lax.broadcasted_iota(jnp.int32, (rows, rows), 1)] * groups, axis=1
        )
        for t in range(n):
            line = epbuf[t, c:c + 1, :]
            column = jnp.sum(jnp.where(eye, line, 0), axis=1, keepdims=True)
            pos_k = t * rows + lax.broadcasted_iota(jnp.int32, (rows, wide), 0)
            seen = jnp.where(pos_k <= pos_q, 1.0, 0.0) * jnp.where(column == mine, 1.0, 0.0)
            allow[c, t * rows:(t + 1) * rows, :] = seen

    loads[4].wait()
    loads[5].wait()

    def compute(p):
        c, g0 = p // per, (p % per) * HP
        at = slot(c)
        for j in range(HP):
            g = g0 + j

            def stack(ref):
                return jnp.concatenate(
                    [
                        ref[at, :, pl.ds(pl.multiple_of((g * groups + i) * DH, DH), DH)]
                        for i in range(groups)
                    ],
                    axis=0,
                )

            q = stack(q_ref)
            do = stack(do_ref)
            key = kvbuf[c, g, :, 0:DH]
            value = kvbuf[c, g, :, DH:2 * DH]
            scores = jnp.where(allow[c] > 0.5, dot(key, q, NT) * scaling, jnp.float32(-1e30))
            top = jnp.max(scores, axis=0, keepdims=True)
            expo = jnp.exp(scores - top)
            probs = expo * (1.0 / jnp.sum(expo, axis=0, keepdims=True))
            dprobs = dot(value, do, NT)
            delta = jnp.sum(probs * dprobs, axis=0, keepdims=True)
            dscores = (probs * (dprobs - delta)).astype(jnp.bfloat16)
            gk = dot(dscores, q, NN)
            gv = dot(probs.astype(jnp.bfloat16), do, NN)
            gown[c, g, :, 0:DH] = gk
            gown[c, g, :, DH:2 * DH] = gv
            gq = (dot(dscores, key, TN) * scaling).astype(jnp.bfloat16)
            for i in range(groups):
                cols = pl.ds(pl.multiple_of((g * groups + i) * DH, DH), DH)
                tq[c, :, cols] = gq[i * rows:(i + 1) * rows]

        @pl.when(c == 0)
        def _():
            trade(0, p, tq, gq_out, groups * DH).start()

        @pl.when(c == 1)
        def _():
            keep(0, p - per, tq, gq_out, groups * DH).start()

    def forward(p):
        for d in reach:
            @pl.when(s >= d)
            def _(d=d):
                up(p, s - d, d).wait_recv()
                if d + 1 in reach:
                    @pl.when(s < n - 1)
                    def _():
                        up(p, s - d, d + 1).start()

    def finish(p):
        c, g0 = p // per, (p % per) * HP
        for d in reversed([0] + reach):
            if d + 1 in reach:
                @pl.when((s >= d) & (s < n - 1))
                def _(d=d):
                    part = (c, pl.ds(g0, HP), chunk(s - d, first(d + 1)))
                    down(p, s - d, d + 1).wait_recv()
                    gown[part] += grecv[part].astype(jnp.float32)
            if d > 0:
                @pl.when(s >= d)
                def _(d=d):
                    part = (c, pl.ds(g0, HP), chunk(s - d, first(d)))
                    gpart[part] = gown[part].astype(jnp.bfloat16)
                    down(p, s - d, d).start()
        for j in range(HP):
            g = g0 + j
            cols = pl.ds(pl.multiple_of(g * DH, DH), DH)
            gk = (gown[c, g, own, 0:DH] * scaling).astype(jnp.bfloat16)
            gv = gown[c, g, own, DH:2 * DH].astype(jnp.bfloat16)

            tk[c, :, cols] = gk
            tv[c, :, cols] = gv

        @pl.when(c == 0)
        def _():
            trade(1, p, tk, gk_out, DH).start()
            trade(2, p, tv, gv_out, DH).start()

        @pl.when(c == 1)
        def _():
            keep(1, p - per, tk, gk_out, DH).start()
            keep(2, p - per, tv, gv_out, DH).start()

    behind = jnp.where(s == n - 1, 0, AHEAD)
    late = behind + LAG * (n - 1 - s)

    def step(i, carry):
        send_own(i + OWN)

        @pl.when(i < pieces)
        def _():
            forward(i)

        @pl.when((i >= behind) & (i < pieces + behind))
        def _():
            compute(i - behind)

        @pl.when((i >= late) & (i < pieces + late))
        def _():
            finish(i - late)
        return carry

    lax.fori_loop(0, pieces + AHEAD + LAG * (n - 1), step, 0)

    def drain(p, carry):
        for d in reach:
            @pl.when((s >= d - 1) & (s < n - 1))
            def _(d=d):
                up(p, s - d + 1, d).wait_send()

            @pl.when(s >= d)
            def _(d=d):
                down(p, s - d, d).wait_send()
        return carry

    lax.fori_loop(0, pieces, drain, 0)
    for t in range(1, n):
        @pl.when(t > s)
        def _(t=t):
            ep_copy(s, t).wait_send()

    def drain_trade(p, carry):
        trade(0, p, tq, gq_out, groups * DH).wait()
        trade(1, p, tk, gk_out, DH).wait()
        trade(2, p, tv, gv_out, DH).wait()
        keep(0, p, tq, gq_out, groups * DH).wait()
        keep(1, p, tk, gk_out, DH).wait()
        keep(2, p, tv, gv_out, DH).wait()
        return carry

    lax.fori_loop(0, per, drain_trade, 0)


def call(n, ndp, mask, send_slot, episodes, queries, key_rows, value_rows, cotangent):
    rows = queries.shape[1]
    heads = key_rows.shape[2] // DH
    groups = queries.shape[2] // key_rows.shape[2]
    pieces = 2 * heads // HP
    dma = pltpu.SemaphoreType.DMA
    return pl.pallas_call(
        functools.partial(kernel, n, ndp, mask),
        out_shape=[
            jax.ShapeDtypeStruct(x.shape, x.dtype) for x in (queries, key_rows, value_rows)
        ],
        in_specs=[pl.BlockSpec(memory_space=pl.ANY)] * 6,
        out_specs=[pl.BlockSpec(memory_space=pl.ANY)] * 3,
        scratch_shapes=[
            pltpu.SMEM(send_slot.shape, jnp.int32),
            pltpu.VMEM(episodes.shape, jnp.int32),
            pltpu.VMEM(queries.shape, jnp.bfloat16),
            pltpu.VMEM(key_rows.shape, jnp.bfloat16),
            pltpu.VMEM(value_rows.shape, jnp.bfloat16),
            pltpu.VMEM(cotangent.shape, jnp.bfloat16),
            dma((6,)),
            dma((3, pieces // 2)),
            pltpu.VMEM((2, heads, n * rows, 2 * DH), jnp.bfloat16),
            pltpu.VMEM((n, 8, DH), jnp.int32),
            pltpu.VMEM((2, n * rows, groups * rows), jnp.float32),
            pltpu.VMEM((2, heads, n * rows, 2 * DH), jnp.bfloat16),
            pltpu.VMEM((2, heads, n * rows, 2 * DH), jnp.float32),
            pltpu.VMEM((2, heads, n * rows, 2 * DH), jnp.bfloat16),
            pltpu.VMEM(queries.shape, jnp.bfloat16),
            pltpu.VMEM(key_rows.shape, jnp.bfloat16),
            pltpu.VMEM(value_rows.shape, jnp.bfloat16),
            dma((pieces, n)),
            dma((pieces, n)),
            dma((n,)),
            dma((n,)),
            dma((pieces, n)),
            dma((pieces, n)),
            dma((3, pieces // 2)),
            dma((3, pieces // 2)),
        ],
        compiler_params=pltpu.CompilerParams(collective_id=mask, has_side_effects=True),
    )(send_slot, episodes, queries, key_rows, value_rows, cotangent)


def emit(a_ref, b_ref, c_ref, a_out, b_out, c_out, sems):
    copies = [
        pltpu.make_async_copy(src, dst, sems.at[i])
        for i, (src, dst) in enumerate(((a_ref, a_out), (b_ref, b_out), (c_ref, c_out)))
    ]
    for copy in copies:
        copy.start()
    for copy in copies:
        copy.wait()


def deliver(*grads):
    return pl.pallas_call(
        emit,
        out_shape=[jax.ShapeDtypeStruct(x.shape, x.dtype) for x in grads],
        in_specs=[pl.BlockSpec(memory_space=pl.ANY)] * 3,
        out_specs=[pl.BlockSpec(memory_space=pl.ANY)] * 3,
        scratch_shapes=[pltpu.SemaphoreType.DMA((3,))],
    )(*grads)


def solution(mesh):
    n, ndp = mesh.shape["seq"], mesh.shape["dp"]

    def per_device(queries, key_rows, value_rows, cotangent, episodes, send_slot, swap_mask):
        return tuple(deliver(*lax.switch(
            swap_mask[0] - 1,
            [functools.partial(call, n, ndp, mask) for mask in range(1, ndp)],
            send_slot, episodes, queries, key_rows, value_rows, cotangent,
        )))

    in_specs = (
        P("dp", "seq", None),
        P("dp", "seq", None),
        P("dp", "seq", None),
        P("dp", "seq", None),
        P("dp", "seq"),
        P("dp"),
        P(),
    )
    out_specs = (P("dp", "seq", None), P("dp", "seq", None), P("dp", "seq", None))
    return jax.shard_map(
        per_device, mesh=mesh, in_specs=in_specs, out_specs=out_specs, check_vma=False
    )
```
